32 devices in a mesh: dp: 4 (over x, core), mp: 8 (over z, y).
Axes of the slice: x: 2, y: 2, z: 4, core: 2. Of those that a mesh axis runs over, the one named last changes fastest.
Arguments:
- tokens: bfloat16 [32768, 768], P(('dp', 'mp')), may hold values from -6 to 6
- lengths: int32 [64], P(('dp', 'mp')), may hold values from 16 to 512, as said below
- w_in: bfloat16 [768, 3072], P('dp', 'mp'), may hold values from -0.21875 to 0.21875
- b_in: bfloat16 [3072], P('mp'), may hold values from -3 to 3
- w_out: bfloat16 [3072, 768], P('mp', 'dp'), may hold values from -0.109375 to 0.109375
- b_out: float32 [768], replicated, may hold values from -2 to 2
- gain_mix: float32 [768], replicated, may hold values from 0.25 to 1.75
- shift_mix: float32 [768], replicated, may hold values from -2 to 2
- gain_ffn: float32 [768], replicated, may hold values from 0.25 to 1.75
- shift_ffn: float32 [768], replicated, may hold values from -2 to 2
- cotangent: bfloat16 [32768, 768], P(('dp', 'mp')), may hold values from -6 to 6
Outputs:
- layer_out: bfloat16 [32768, 768], P(('dp', 'mp'))
- grad_tokens: bfloat16 [32768, 768], P(('dp', 'mp'))
- grad_w_in: float32 [768, 3072], P('dp', 'mp')
- grad_b_in: float32 [3072], replicated
- grad_w_out: float32 [3072, 768], P('mp', 'dp')
- grad_b_out: float32 [768], replicated
- grad_gain_mix: float32 [768], replicated
- grad_shift_mix: float32 [768], replicated
- grad_gain_ffn: float32 [768], replicated
- grad_shift_ffn: float32 [768], replicated
The draws below stay inside these ranges and needn't reach their ends.
Inputs may be any that keep to these rules, and one draw needn't show every extreme that they name: `lengths`: in every aligned block of 8 items exactly one has length 512; the others have at most 256.
All inputs are finite; a program needn't handle non-finite values.
Results may differ from the reference program's by a relative error of at most 0.0095.
Values may be sent and summed in bfloat16 or wider, within the bound.
No kernel may reach another device: no remote copies, remote signals or barrier semaphores. Data moves between devices by JAX's collectives and lax.ppermute only.
A program may use at most 320 MiB of HBM per device.

```python
import math
import jax
import jax.numpy as jnp
from jax import lax

D = 768
FF = 3072
LEN = 512
SEQS = 64
TOKENS = 32768


def draw_lengths(key, part):
    key_base, key_pick = jax.random.split(key)
    lowest = max(1, LEN // 32)
    base = jax.random.randint(key_base, (SEQS,), lowest, LEN // 2 + 1)
    chosen = jax.random.randint(key_pick, (SEQS // 8,), 0, 8)
    within = jnp.arange(SEQS, dtype=jnp.int32).reshape(SEQS // 8, 8) % 8
    picked = (within == chosen[:, None]).reshape(SEQS)
    return jnp.where(picked, LEN, base).astype(jnp.int32)


def level_of(key, extent, pieces, low, top_value):
    def one(axis_at, shards_of):
        heights = jax.random.uniform(jax.random.fold_in(jax.random.fold_in(key, 6), axis_at), (shards_of,), jnp.float32, low / len(pieces), top_value / len(pieces))
        return jnp.repeat(jnp.exp(heights), extent[axis_at] // shards_of).reshape((-1,) + (1,) * (len(extent) - axis_at - 1))

    factor_of = one(*pieces[0])
    for cut in pieces[1:]:
        factor_of = factor_of * one(*cut)
    return factor_of


def centred(own_key, shape, scale, limit, pieces=(), kind=jnp.bfloat16):
    values = scale * jax.random.normal(own_key, shape, jnp.float32)
    if pieces:
        values = values * level_of(own_key, shape, pieces, -0.22, 0.18)
    return jnp.clip(values, -limit, limit).astype(kind)


def setup_inputs(seed: int = 0) -> dict:
    key_of = jax.random.split(jax.random.key(seed), 12)
    tokens = centred(key_of[0], (TOKENS, D), 1.0, 6.0, ((0, 32),))
    lengths = draw_lengths(jax.random.fold_in(key_of[11], 71), 0)
    w_in = centred(key_of[2], (D, FF), D ** -0.5, 0.21875, ((0, 4), (1, 8)))
    b_in = centred(key_of[3], (FF,), 0.5, 3.0, ((0, 8),))
    w_out = centred(key_of[4], (FF, D), FF ** -0.5, 0.109375, ((0, 8), (1, 4)))
    b_out = centred(key_of[5], (D,), 0.3, 2.0, (), jnp.float32)
    gain_mix = jnp.clip(1.0 + 0.15 * jax.random.normal(key_of[6], (D,), jnp.float32), 0.25, 1.75)
    shift_mix = centred(key_of[7], (D,), 0.3, 2.0, (), jnp.float32)
    gain_ffn = jnp.clip(1.0 + 0.15 * jax.random.normal(key_of[8], (D,), jnp.float32), 0.25, 1.75)
    shift_ffn = centred(key_of[9], (D,), 0.3, 2.0, (), jnp.float32)
    cotangent = centred(key_of[10], (TOKENS, D), 1.0, 6.0, ((0, 32),))
    return dict(tokens=tokens, lengths=lengths, w_in=w_in, b_in=b_in, w_out=w_out, b_out=b_out, gain_mix=gain_mix, shift_mix=shift_mix, gain_ffn=gain_ffn, shift_ffn=shift_ffn, cotangent=cotangent)


@jax.custom_vjp
def low(v):
    return lax.optimization_barrier(v.astype(jnp.bfloat16)).astype(jnp.float32)

@jax.custom_vjp
def low_back(v):
    return v

def low_keep(v):
    return (low(v), None)

def low_pass(kept, grad):
    return (grad,)

def back_keep(v):
    return (v, None)

def back_low(kept, grad):
    return (low(grad),)
low.defvjp(low_keep, low_pass)
low_back.defvjp(back_keep, back_low)
epsilon = 1e-06

def dft_tables(width):
    index = jnp.arange(width, dtype=jnp.int32)
    phase = index[:, None] * index[None, :] % width
    angle = phase.astype(jnp.float32) * (2.0 * math.pi / width)
    factor = 1.0 / math.sqrt(width)
    return (jnp.cos(angle) * factor, jnp.sin(angle) * factor)

def layer_norm(values, gain, shift):
    center = values - lax.optimization_barrier(jnp.mean(values, axis=-1, keepdims=True))
    spread = lax.optimization_barrier(jnp.mean(center * center, axis=-1, keepdims=True))
    return center * lax.rsqrt(spread + epsilon) * gain + shift

def block(inputs, live_mask, feat_table, seq_table, w_in, b_in, w_out, b_out, gain_mix, shift_mix, gain_ffn, shift_ffn):
    highest = lax.Precision.HIGHEST
    masked = inputs * live_mask
    spectra = low(low_back(jnp.einsum('gtd,de->gte', masked, feat_table, precision=highest)))
    width = masked.shape[-1]
    stacked = jnp.concatenate([spectra[..., :width], spectra[..., width:]], axis=1)
    mixed = low_back(jnp.einsum('st,gtd->gsd', seq_table, stacked, precision=highest))
    first = layer_norm(masked + mixed, gain_mix, shift_mix)
    pre_act = low_back(jnp.einsum('gtd,df->gtf', low(first), w_in, precision=highest) + b_in)
    hidden = low(jax.nn.gelu(pre_act))
    branch = low_back(jnp.einsum('gtf,fd->gtd', hidden, w_out, precision=highest) + b_out)
    return live_mask * layer_norm(first + branch, gain_ffn, shift_ffn)

def reference(tokens, lengths, w_in, b_in, w_out, b_out, gain_mix, shift_mix, gain_ffn, shift_ffn, cotangent):
    cos_feat, sin_feat = dft_tables(D)
    feat_table = low(jnp.concatenate([cos_feat, sin_feat], axis=1))
    cos_seq, sin_seq = dft_tables(LEN)
    seq_table = low(jnp.concatenate([cos_seq, -sin_seq], axis=1))
    group = math.gcd(SEQS, max(1, 4096 // LEN))
    blocks_count = SEQS // group
    input_blocks = tokens.astype(jnp.float32).reshape(blocks_count, group, LEN, D)
    cot_blocks = cotangent.astype(jnp.float32).reshape(blocks_count, group, LEN, D)
    length_blocks = lengths.reshape(blocks_count, group)
    params = (w_in.astype(jnp.float32), b_in.astype(jnp.float32), w_out.astype(jnp.float32), b_out.astype(jnp.float32), gain_mix.astype(jnp.float32), shift_mix.astype(jnp.float32), gain_ffn.astype(jnp.float32), shift_ffn.astype(jnp.float32))
    positions = jnp.arange(LEN, dtype=jnp.int32)

    def step(totals, item):
        inputs, cot_part, item_lengths = item
        live_mask = (positions[None, :] < item_lengths[:, None]).astype(jnp.float32)[..., None]

        def apply_all(values, *weights):
            return block(values, live_mask, feat_table, seq_table, *weights)
        result, pull = jax.vjp(apply_all, inputs, *params)
        grads = pull(cot_part)
        totals = tuple((total + grad for total, grad in zip(totals, grads[1:])))
        return (totals, (result.astype(jnp.bfloat16), grads[0].astype(jnp.bfloat16)))
    start = tuple((jnp.zeros_like(param) for param in params))
    totals, (results, input_grads) = lax.scan(step, start, (input_blocks, cot_blocks, length_blocks))
    return (results.reshape(TOKENS, D), input_grads.reshape(TOKENS, D), totals[0], totals[1], totals[2], totals[3], totals[4], totals[5], totals[6], totals[7])
```

```python
from functools import partial
import math

import jax
import jax.numpy as jnp
from jax import lax
from jax.experimental import pallas as pl
from jax.experimental.pallas import tpu as pltpu
from jax.sharding import PartitionSpec as P

D = 768
FF = 3072
LEN = 512
HALF = LEN // 2
ROWS = LEN + HALF

epsilon = 1e-06
GELU_C = math.sqrt(2.0 / math.pi)


def dft_tables(width):
    index = jnp.arange(width, dtype=jnp.int32)
    phase = index[:, None] * index[None, :] % width
    angle = phase.astype(jnp.float32) * (2.0 * math.pi / width)
    factor = 1.0 / math.sqrt(width)
    return (jnp.cos(angle) * factor, jnp.sin(angle) * factor)


def layer_norm(values, gain, shift):
    center = values - jnp.mean(values, axis=-1, keepdims=True)
    spread = jnp.mean(center * center, axis=-1, keepdims=True)
    return center * lax.rsqrt(spread + epsilon) * gain + shift


def masked_norm(values, gain, shift, live_mask):
    return live_mask * layer_norm(values, gain, shift)


def inner_rows(left, right):
    return lax.dot_general(
        left, right, (((1,), (1,)), ((), ())), preferred_element_type=jnp.float32
    )


def dot(left, right):
    return jnp.dot(left, right, preferred_element_type=jnp.float32)


def forward_kernel(first_ref, weights_ref, bias_ref, pre_ref, branch_ref):
    width = pre_ref.shape[-1]
    chunk = pl.program_id(0)

    @pl.when(chunk == 0)
    def _():
        branch_ref[...] = jnp.zeros_like(branch_ref)

    pre = dot(first_ref[...], weights_ref[0, :, :width]) + bias_ref[0]
    pre_ref[0] = pre
    inner = jnp.tanh(GELU_C * (pre + 0.044715 * (pre * pre * pre)))
    hidden = (0.5 * pre * (1.0 + inner)).astype(jnp.bfloat16)
    branch_ref[...] += inner_rows(hidden, weights_ref[0, :, width:])


def backward_kernel(
    grad_ref, grad_turned_ref, first_turned_ref, weights_ref, pre_ref, grad_w_ref, bias_ref, ffn_ref
):
    width = pre_ref.shape[-1]
    chunk = pl.program_id(0)

    @pl.when(chunk == 0)
    def _():
        ffn_ref[...] = jnp.zeros_like(ffn_ref)

    grad_hidden = dot(grad_ref[...], weights_ref[0, :, width:])
    pre = pre_ref[0]
    square = pre * pre
    inner = jnp.tanh(GELU_C * (pre + 0.044715 * (square * pre)))
    outer = 0.5 * (1.0 + inner)
    hidden = (pre * outer).astype(jnp.bfloat16)
    slope = outer + (0.5 * GELU_C) * pre * (1.0 - inner * inner) * (1.0 + (3 * 0.044715) * square)
    grad_pre = (grad_hidden * slope).astype(jnp.bfloat16)
    bias_ref[0] = jnp.sum(grad_pre.astype(jnp.float32), axis=0, keepdims=True)
    grad_w_ref[0, :, width:] = dot(grad_turned_ref[...], hidden).astype(jnp.bfloat16)
    grad_w_ref[0, :, :width] = dot(first_turned_ref[...], grad_pre).astype(jnp.bfloat16)
    ffn_ref[...] += inner_rows(grad_pre, weights_ref[0, :, :width])


def whole(shape):
    return pl.BlockSpec(shape, lambda m: (0,) * len(shape))


def chunked(shape):
    return pl.BlockSpec((1,) + shape, lambda m: (m,) + (0,) * len(shape))


def feed_forward(first_low, weights, bias):
    chunks, _, both = weights.shape
    width = both // 2
    rows = first_low.shape[0]
    return pl.pallas_call(
        forward_kernel,
        grid=(chunks,),
        in_specs=[whole((rows, D)), chunked((D, both)), chunked((1, width))],
        out_specs=[chunked((rows, width)), whole((rows, D))],
        out_shape=[
            jax.ShapeDtypeStruct((chunks, rows, width), jnp.float32),
            jax.ShapeDtypeStruct((rows, D), jnp.float32),
        ],
        cost_estimate=pl.CostEstimate(
            flops=4 * rows * D * width * chunks,
            bytes_accessed=chunks * (2 * D * both + 4 * rows * width) + 6 * rows * D,
            transcendentals=rows * width * chunks,
        ),
        name="ffn_forward",
    )(first_low, weights, bias)


def feed_backward(grad_branch, first_low, weights, pre):
    chunks, rows, width = pre.shape
    both = 2 * width
    return pl.pallas_call(
        backward_kernel,
        grid=(chunks,),
        in_specs=[
            whole((rows, D)),
            whole((D, rows)),
            whole((D, rows)),
            chunked((D, both)),
            chunked((rows, width)),
        ],
        out_specs=[chunked((D, both)), chunked((1, width)), whole((rows, D))],
        out_shape=[
            jax.ShapeDtypeStruct((chunks, D, both), jnp.bfloat16),
            jax.ShapeDtypeStruct((chunks, 1, width), jnp.float32),
            jax.ShapeDtypeStruct((rows, D), jnp.float32),
        ],
        cost_estimate=pl.CostEstimate(
            flops=8 * rows * D * width * chunks,
            bytes_accessed=chunks * (4 * D * both + 4 * rows * width) + 10 * rows * D,
            transcendentals=rows * width * chunks,
        ),
        name="ffn_backward",
    )(grad_branch, grad_branch.T, first_low.T, weights, pre)


def flips(size):
    bit = 1
    while bit < size:
        yield bit, [(i, i ^ bit) for i in range(size)]
        bit *= 2


def body(
    sizes,
    tokens, lengths, w_in, b_in, w_out, b_out, gain_mix, shift_mix, gain_ffn, shift_ffn, cotangent,
):
    width = w_in.shape[1]
    parts = sizes["mp"]
    shard = jnp.concatenate([w_in, w_out.T], axis=1)
    weights = lax.all_gather(shard, ("mp", "dp"), axis=0, tiled=True).reshape(parts, D, 2 * width)
    held = b_in.astype(jnp.bfloat16)[None]
    for _, pairs in flips(parts):
        held = jnp.concatenate([held, lax.ppermute(held, "mp", pairs)], axis=0)
    order = jnp.arange(parts, dtype=jnp.int32) ^ lax.axis_index("mp")
    bias = held[order].astype(jnp.float32)[:, None, :]

    long = jnp.where(lengths[0] > HALF, 0, 1)
    lens = (lengths[long], lengths[1 - long])
    starts = (long * LEN, (1 - long) * LEN)

    def take(values):
        return jnp.concatenate(
            [
                lax.dynamic_slice_in_dim(values, starts[0], LEN, axis=0),
                lax.dynamic_slice_in_dim(values, starts[1], HALF, axis=0),
            ],
            axis=0,
        )

    def put(values):
        head, tail = values[:LEN], values[LEN:]
        rest = jnp.zeros((HALF, D), values.dtype)
        return jnp.where(
            long == 0,
            jnp.concatenate([head, tail, rest], axis=0),
            jnp.concatenate([tail, rest, head], axis=0),
        )

    spots = jnp.concatenate([jnp.arange(LEN, dtype=jnp.int32), jnp.arange(HALF, dtype=jnp.int32)])
    limits = jnp.where(jnp.arange(ROWS) < LEN, lens[0], lens[1])
    live_mask = (spots < limits).astype(jnp.float32)[:, None]

    cos_feat, sin_feat = dft_tables(D)
    feat_table = jnp.concatenate([cos_feat, sin_feat], axis=1).astype(jnp.bfloat16)
    cos_seq, sin_seq = dft_tables(LEN)
    cos_low, sin_low = cos_seq.astype(jnp.bfloat16), (-sin_seq).astype(jnp.bfloat16)
    seq_long = jnp.concatenate([cos_low, sin_low], axis=1)
    seq_short = jnp.concatenate([cos_low[:HALF, :HALF], sin_low[:HALF, :HALF]], axis=1)

    masked = take(tokens) * live_mask.astype(jnp.bfloat16)
    spectra = dot(masked, feat_table).astype(jnp.bfloat16)

    def stack(values):
        return jnp.concatenate([values[:, :D], values[:, D:]], axis=0)

    mixed = jnp.concatenate(
        [dot(seq_long, stack(spectra[:LEN])), dot(seq_short, stack(spectra[LEN:]))], axis=0
    )
    first, first_back = jax.vjp(layer_norm, masked.astype(jnp.float32) + mixed, gain_mix, shift_mix)
    first_low = first.astype(jnp.bfloat16)
    pre, branch = feed_forward(first_low, weights, bias)
    result, last_back = jax.vjp(
        partial(masked_norm, live_mask=live_mask), first + (branch + b_out), gain_ffn, shift_ffn
    )
    layer_out = put(result.astype(jnp.bfloat16))
    grad_second, grad_gain_ffn, grad_shift_ffn = last_back(take(cotangent).astype(jnp.float32))
    grad_branch = grad_second.astype(jnp.bfloat16)
    grad_b_out = jnp.sum(grad_branch.astype(jnp.float32), axis=0)
    grad_w, grad_bias, grad_ffn = feed_backward(grad_branch, first_low, weights, pre)
    grad_shard = lax.psum_scatter(
        grad_w.reshape(parts * D, 2 * width), ("mp", "dp"), scatter_dimension=0, tiled=True
    ).astype(jnp.float32)
    grad_sum, grad_gain_mix, grad_shift_mix = first_back(grad_second + grad_ffn)
    grad_mixed = grad_sum.astype(jnp.bfloat16)

    def back(table, values):
        turned = lax.dot_general(
            table, values, (((0,), (0,)), ((), ())), preferred_element_type=jnp.float32
        ).astype(jnp.bfloat16)
        count = values.shape[0]
        return jnp.concatenate([turned[:count], turned[count:]], axis=1)

    grad_spectra = jnp.concatenate(
        [back(seq_long, grad_mixed[:LEN]), back(seq_short, grad_mixed[LEN:])], axis=0
    )
    grad_masked = grad_sum + inner_rows(grad_spectra, feat_table)
    grad_tokens = put((grad_masked * live_mask).astype(jnp.bfloat16))

    totals = jnp.concatenate(
        [grad_bias.reshape(-1), grad_b_out, grad_gain_mix, grad_shift_mix, grad_gain_ffn, grad_shift_ffn]
    )
    for axis in ("dp", "mp"):
        for _, pairs in flips(sizes[axis]):
            totals = totals + lax.ppermute(totals, axis, pairs)
    sums = [totals[FF + i * D : FF + (i + 1) * D] for i in range(5)]
    return (
        layer_out,
        grad_tokens,
        grad_shard[:, :width],
        totals[:FF],
        grad_shard[:, width:].T,
        *sums,
    )


def solution(mesh):
    rows = P(("dp", "mp"), None)
    return jax.shard_map(
        partial(body, dict(mesh.shape)),
        mesh=mesh,
        in_specs=(
            rows, P(("dp", "mp")), P("dp", "mp"), P("mp"), P("mp", "dp"),
            P(), P(), P(), P(), P(), rows,
        ),
        out_specs=(rows, rows, P("dp", "mp"), P(), P("mp", "dp"), P(), P(), P(), P(), P()),
        check_vma=False,
    )
```
